256 devices in a mesh: block: 16 (over z_hi, y), tok: 16 (over z_lo, x, core).
Axes of the slice: x: 4, y: 4, z: 8 (z_hi: 4, z_lo: 2; z = z_hi * 2 + z_lo), core: 2. Of those that a mesh axis runs over, the one named last changes fastest.
Arguments:
- queries: bfloat16 [262144, 512], P(('block', 'tok')), may hold values from -6 to 6
- keys: bfloat16 [262144, 512], P(('block', 'tok')), may hold values from -6 to 6
- values: bfloat16 [262144, 512], P(('block', 'tok')), may hold values from -6 to 6
- rates: float32 [3, 262144], P(None, ('block', 'tok')), may hold values from 0.3 to 3
- fast0: float32 [3, 512, 512], replicated, may hold values from -1 to 1
Outputs:
- outputs: bfloat16 [262144, 512], P(('block', 'tok'))
The draws below stay inside these ranges and needn't reach their ends.
All inputs are finite; a program needn't handle non-finite values.
Results may differ from the reference program's by a relative error of at most 0.039.
Values may be sent and summed in bfloat16 or wider, within the bound.
No kernel may reach another device: no remote copies, remote signals or barrier semaphores. Data moves between devices by JAX's collectives and lax.ppermute only.
A program may use at most 128 MiB of HBM per device.

```python
import math
import jax
import jax.numpy as jnp
from jax import lax

D = 512
HID = 512
TOK_DEV = 1024
TOKENS = 262144
N_BLOCK = 16
N_TOK = 16


def draw_fast0(key, part):
    first, second = jax.random.split(jax.random.fold_in(key, 11), 2)
    scales = jnp.exp(jax.random.uniform(first, (3, HID, 1), jnp.float32, jnp.log(2.0), jnp.log(2.5)))
    fan_scale = jnp.array([D, D, HID], jnp.float32).reshape(3, 1, 1) ** (-0.5)
    entries = jnp.clip(jax.random.normal(second, (3, HID, D), jnp.float32), -4.0, 4.0)
    return jnp.clip(entries * scales * fan_scale, -1.0, 1.0).astype(jnp.float32)


def level_of(own_key, shape, cuts, smallest, top_value):
    def one(dim, blocks):
        draws = jax.random.uniform(jax.random.fold_in(jax.random.fold_in(own_key, 6), dim), (blocks,), jnp.float32, smallest / len(cuts), top_value / len(cuts))
        return jnp.repeat(jnp.exp(draws), shape[dim] // blocks).reshape((-1,) + (1,) * (len(shape) - dim - 1))

    factor_of = one(*cuts[0])
    for cut in cuts[1:]:
        factor_of = factor_of * one(*cut)
    return factor_of


def gaussian(key, dims, width, most, cuts=(), held_as=jnp.bfloat16):
    values = jax.random.normal(key, dims, jnp.float32) * width
    if len(cuts) > 0:
        values = level_of(key, dims, cuts, -0.22, 0.18) * values
    return jnp.clip(values, min=-most, max=most).astype(held_as)


def setup_inputs(seed: int = 0) -> dict:
    splits = jax.random.split(jax.random.key(seed), 6)
    return {
        "queries": gaussian(splits[0], (TOKENS, D), 1.0, 6.0, ((0, 256),)),
        "keys": gaussian(splits[1], (TOKENS, D), 1.0, 6.0, ((0, 256),)),
        "values": gaussian(splits[2], (TOKENS, D), 1.0, 6.0, ((0, 256),)),
        "rates": jnp.clip(jnp.exp(math.log(3.0) - 2.3025851 * jax.random.uniform(splits[3], (3, TOKENS), jnp.float32) ** level_of(splits[3], (3, TOKENS), ((1, 256),), -0.2, 0.2)), 0.3, 3.0),
        "fast0": draw_fast0(jax.random.fold_in(splits[5], 71), 0),
    }


def contract_cols(left, right):
    return lax.dot_general(left, right, (((1,), (1,)), ((), ())), preferred_element_type=jnp.float32)

def contract_rows(left, right):
    return lax.dot_general(left, right, (((0,), (0,)), ((), ())), preferred_element_type=jnp.float32)

def rescale(rows, target):
    return rows * (target / jnp.sqrt(lax.optimization_barrier(jnp.sum(rows * rows, -1, keepdims=True)) + 1e-06))

def fast_grads(weight_bf, keys, values, rates, scale):
    gate = contract_cols(keys, weight_bf[0])
    upper = contract_cols(keys, weight_bf[1])
    sigma = jax.nn.sigmoid(gate)
    active = gate * sigma
    hidden = active * upper
    back = -contract_cols(values, weight_bf[2])
    dgate = back * upper * sigma * (1.0 + gate * (1.0 - sigma))
    dupper = back * active
    rate = rates * scale
    grad_gate = contract_rows((rate[0][:, None] * dgate).astype(jnp.bfloat16), keys)
    grad_up = contract_rows((rate[1][:, None] * dupper).astype(jnp.bfloat16), keys)
    grad_down = -contract_rows((rate[2][:, None] * hidden).astype(jnp.bfloat16), values)
    return jnp.stack([grad_gate, grad_up, grad_down])

def apply_fast(weight_bf, queries):
    gate = contract_cols(queries, weight_bf[0])
    upper = contract_cols(queries, weight_bf[1])
    hidden = (jax.nn.silu(gate) * upper).astype(jnp.bfloat16)
    return jnp.dot(hidden, weight_bf[2], preferred_element_type=jnp.float32).astype(jnp.bfloat16)

def reference(queries, keys, values, rates, fast0):
    segment = TOK_DEV * N_TOK
    scale = (segment * D) ** (-0.5)
    target = jnp.sqrt(lax.optimization_barrier(jnp.sum(fast0 * fast0, -1, keepdims=True)))

    def segment_delta(index):
        seg_keys = lax.dynamic_slice_in_dim(keys, index * segment, segment, 0)
        seg_values = lax.dynamic_slice_in_dim(values, index * segment, segment, 0)
        seg_rates = lax.dynamic_slice_in_dim(rates, index * segment, segment, 1)
        weights = fast0
        for update_step in range(2):
            weight_bf = weights.astype(jnp.bfloat16)

            def shard_term(shard):
                start = shard * TOK_DEV
                return fast_grads(weight_bf, lax.dynamic_slice_in_dim(seg_keys, start, TOK_DEV, 0), lax.dynamic_slice_in_dim(seg_values, start, TOK_DEV, 0), lax.dynamic_slice_in_dim(seg_rates, start, TOK_DEV, 1), scale)
            partials = lax.map(shard_term, jnp.arange(N_TOK, dtype=jnp.int32))
            rounded = lax.optimization_barrier(partials.astype(jnp.bfloat16))
            total = lax.optimization_barrier(jnp.sum(rounded.astype(jnp.float32), 0))
            weights = rescale(weights - total, target)
        return weights - fast0
    deltas = lax.map(segment_delta, jnp.arange(N_BLOCK, dtype=jnp.int32))
    prefix = jnp.cumsum(deltas, 0)
    applied = rescale(fast0[None] + prefix, target[None])

    def segment_out(pair):
        return apply_fast(pair[0].astype(jnp.bfloat16), pair[1])
    outputs = lax.map(segment_out, (applied, queries.reshape(N_BLOCK, segment, D)))
    return outputs.reshape(TOKENS, D)
```

```python
import jax
import jax.numpy as jnp
from jax import lax
from jax.experimental import pallas as pl
from jax.experimental.pallas import tpu as pltpu
from jax.sharding import PartitionSpec as P

F32, BF16 = jnp.float32, jnp.bfloat16
VMEM = pl.BlockSpec(memory_space=pltpu.VMEM)
ANY = pl.BlockSpec(memory_space=pl.ANY)
TILE = 512
PEERS = 8


def nt(a, b):
    return lax.dot_general(a, b, (((1,), (1,)), ((), ())), preferred_element_type=F32)


def nn(a, b):
    return lax.dot_general(a, b, (((1,), (0,)), ((), ())), preferred_element_type=F32)


def factors(weights, keys, values, rates, scale):
    gate, upper, back = nt(weights[0], keys), nt(weights[1], keys), -nt(weights[2], values)
    sigma = jax.nn.sigmoid(gate)
    active = gate * sigma
    rates = rates * scale
    dgate = back * upper * sigma * (1.0 + gate * (1.0 - sigma))
    return (
        (rates[0:1] * dgate).astype(BF16),
        (rates[1:2] * (back * active)).astype(BF16),
        (-(rates[2:3] * (active * upper))).astype(BF16),
    )


def fill_factors(out, weights, keys, values, rates, scale, start):
    for at in range(0, keys.shape[0], TILE):
        part = factors(weights, keys[at : at + TILE], values[at : at + TILE], rates[:, at : at + TILE], scale)
        for i in range(3):
            out[i, :, start + at : start + at + TILE] = part[i]


def rescale(rows, target):
    return rows * (target / jnp.sqrt(jnp.sum(rows * rows, -1, keepdims=True) + 1e-06))


def norm(rows):
    return jnp.sqrt(jnp.sum(rows * rows, -1, keepdims=True))


def call(kernel, outs, args, scratch=(), specs=None, flops=0):
    size = sum(a.size * a.dtype.itemsize for a in (*args, *outs))
    return pl.pallas_call(
        kernel,
        out_shape=list(outs),
        in_specs=specs or [VMEM] * len(args),
        out_specs=[VMEM] * len(outs),
        scratch_shapes=list(scratch),
        cost_estimate=pl.CostEstimate(flops=flops, bytes_accessed=size, transcendentals=0),
    )(*args)


def shape(dims, dtype):
    return jax.ShapeDtypeStruct(dims, dtype)


def shards(queries, keys, values, rates, fast0):
    tokens, width = keys.shape
    hidden = fast0.shape[1]
    half, piece = hidden // 2, hidden // 16
    scale = (tokens * lax.axis_size("tok") * width) ** (-0.5)
    piece_bf, piece_f32 = shape((3, piece, width), BF16), shape((3, piece, width), F32)
    flops = 12 * tokens * width * half

    def swap(value):
        return lax.ppermute(value, "tok", [(t, t ^ 1) for t in range(16)])

    def to_peer(value, k):
        return lax.ppermute(value, "tok", [(t, t ^ (2 * k)) for t in range(16)])

    def along_block(value, k):
        return lax.ppermute(value, "block", [(b, b ^ k) for b in range(16)])

    other_keys, other_values, other_rates = swap(keys), swap(values), swap(rates)

    def first(fast0_ref, keys_ref, values_ref, rates_ref, weights_ref, own_ref, total_ref, rows, left, sem):
        place = lax.axis_index("tok")
        chip, core = place // 2, place % 2
        copies = []
        for k in range(PEERS):
            begin = pl.multiple_of(core * half + (chip ^ k) * piece, piece)
            copies.append(pltpu.make_async_copy(fast0_ref.at[:, pl.ds(begin, piece)], rows.at[k], sem.at[k]))
            copies[-1].start()
        for k in range(PEERS):
            copies[k].wait()
            weights_ref[:, k * piece : (k + 1) * piece] = rows[k].astype(BF16)
        own_ref[...] = rows[0]
        weights = [weights_ref[i] for i in range(3)]
        fill_factors(left, weights, keys_ref, values_ref, rates_ref, scale, 0)
        for i in range(3):
            total_ref[i] = nn(left[i], (keys_ref if i < 2 else values_ref)[...])

    weights, own, total = call(
        first,
        [shape((3, half, width), BF16), piece_f32, shape((3, half, width), F32)],
        (fast0, keys, values, rates),
        [pltpu.VMEM((PEERS, 3, piece, width), F32), pltpu.VMEM((3, half, tokens), BF16), pltpu.SemaphoreType.DMA((PEERS,))],
        [ANY, VMEM, VMEM, VMEM],
        flops,
    )

    def second(weights_ref, keys_ref, values_ref, rates_ref, total_ref, *rest):
        pieces, left = rest[:PEERS], rest[PEERS]
        weights = [weights_ref[i] for i in range(3)]
        fill_factors(left, weights, keys_ref, values_ref, rates_ref, scale, 0)
        for i in range(3):
            grad = total_ref[i] + nn(left[i], (keys_ref if i < 2 else values_ref)[...])
            for k in range(PEERS):
                pieces[k][i] = grad[k * piece : (k + 1) * piece].astype(BF16)

    grads = call(
        second,
        [piece_bf] * PEERS,
        (weights, other_keys, other_values, other_rates, total),
        [pltpu.VMEM((3, half, tokens), BF16)],
        flops=flops,
    )

    def spread(pieces):
        return [pieces[0]] + [to_peer(pieces[k], k) for k in range(1, PEERS)]

    def summed(parts):
        total = parts[0][...].astype(F32)
        for part in parts[1:]:
            total = total + part[...].astype(F32)
        return total

    def update_one(own_ref, *rest):
        parts, (new_ref, new_bf_ref) = rest[:PEERS], rest[PEERS:]
        rows = own_ref[...]
        new = rescale(rows - summed(parts), norm(rows))
        new_ref[...] = new
        new_bf_ref[...] = new.astype(BF16)

    new, new_bf = call(update_one, [piece_f32, piece_bf], (own, *spread(grads)))
    gathered = spread([new_bf] * PEERS)

    def again(*refs):
        shard_refs = refs[:PEERS]
        keys_ref, values_ref, rates_ref, keys2_ref, values2_ref, rates2_ref = refs[PEERS : PEERS + 6]
        pieces, left, weights_ref = refs[PEERS + 6 : 2 * PEERS + 6], refs[-2], refs[-1]
        for k in range(PEERS):
            weights_ref[:, k * piece : (k + 1) * piece] = shard_refs[k][...]
        weights = [weights_ref[i] for i in range(3)]
        fill_factors(left, weights, keys_ref, values_ref, rates_ref, scale, 0)
        fill_factors(left, weights, keys2_ref, values2_ref, rates2_ref, scale, tokens)
        for i in range(3):
            right = (keys_ref, keys2_ref) if i < 2 else (values_ref, values2_ref)
            grad = nn(left[i, :, :tokens], right[0][...]) + nn(left[i, :, tokens:], right[1][...])
            for k in range(PEERS):
                pieces[k][i] = grad[k * piece : (k + 1) * piece].astype(BF16)

    grads = call(
        again,
        [piece_bf] * PEERS,
        (*gathered, keys, values, rates, other_keys, other_values, other_rates),
        [pltpu.VMEM((3, half, 2 * tokens), BF16), pltpu.VMEM((3, half, width), BF16)],
        flops=2 * flops,
    )

    def update_two(own_ref, new_ref, *rest):
        parts, (change_ref, change_bf_ref) = rest[:PEERS], rest[PEERS:]
        rows = own_ref[...]
        change = rescale(new_ref[...] - summed(parts), norm(rows)) - rows
        change_ref[...] = change
        change_bf_ref[...] = change.astype(BF16)

    change, change_bf = call(update_two, [piece_f32, piece_bf], (own, new, *spread(grads)))

    def near(change_ref, *rest):
        parts, (prefix_ref, ring_ref) = rest[:3], rest[3:]
        here = lax.axis_index("block") % 4
        prefix, ring = change_ref[...], change_ref[...]
        for k in range(1, 4):
            part = parts[k - 1][...].astype(F32)
            ring = ring + part
            prefix = prefix + jnp.where((here ^ k) < here, part, 0.0)
        prefix_ref[...] = prefix
        ring_ref[...] = ring.astype(BF16)

    prefix, ring = call(
        near, [piece_f32, piece_bf], (change, *[along_block(change_bf, k) for k in range(1, 4)])
    )

    def far(own_ref, prefix_ref, *rest):
        parts, applied_ref = rest[:3], rest[3]
        here = lax.axis_index("block") // 4
        prefix, rows = prefix_ref[...], own_ref[...]
        for k in range(1, 4):
            prefix = prefix + jnp.where((here ^ k) < here, parts[k - 1][...].astype(F32), 0.0)
        applied_ref[...] = rescale(rows + prefix, norm(rows)).astype(BF16)

    (applied,) = call(far, [piece_bf], (own, prefix, *[along_block(ring, 4 * k) for k in range(1, 4)]))

    mine = spread([applied] * PEERS)
    theirs = [swap(part) for part in mine]

    def apply_half(queries, part_refs):
        rows = [jnp.concatenate([ref[i] for ref in part_refs], 0) for i in range(3)]
        gate, upper = nt(queries, rows[0]), nt(queries, rows[1])
        return nn((jax.nn.silu(gate) * upper).astype(BF16), rows[2])

    def apply_mine(queries_ref, *rest):
        for at in range(0, tokens, TILE):
            rest[-1][at : at + TILE] = apply_half(queries_ref[at : at + TILE], rest[:-1])

    def apply_theirs(queries_ref, partial_ref, *rest):
        for at in range(0, tokens, TILE):
            rows = slice(at, at + TILE)
            rest[-1][rows] = (partial_ref[rows] + apply_half(queries_ref[rows], rest[:-1])).astype(BF16)

    (partial,) = call(apply_mine, [shape((tokens, width), F32)], (queries, *mine), flops=flops // 2)
    (outputs,) = call(apply_theirs, [shape((tokens, width), BF16)], (queries, partial, *theirs), flops=flops // 2)
    return outputs


def solution(mesh):
    return jax.shard_map(
        shards,
        mesh=mesh,
        in_specs=(
            P(("block", "tok"), None),
            P(("block", "tok"), None),
            P(("block", "tok"), None),
            P(None, ("block", "tok")),
            P(),
        ),
        out_specs=P(("block", "tok"), None),
        check_vma=False,
    )
```

```python
import jax
import jax.numpy as jnp
from jax import lax
from jax.experimental import pallas as pl
from jax.experimental.pallas import tpu as pltpu
from jax.sharding import PartitionSpec as P

F32, BF16 = jnp.float32, jnp.bfloat16
VMEM = pl.BlockSpec(memory_space=pltpu.VMEM)
HBM = pl.BlockSpec(memory_space=pltpu.HBM)
TILE = 512
PEERS = 8
RING = (1, 3, 2)
PLACES = (0, 1, 3, 4, 2, 5, 7, 6)


def nt(a, b):
    return lax.dot_general(a, b, (((1,), (1,)), ((), ())), preferred_element_type=F32)


def nn(a, b):
    return lax.dot_general(a, b, (((1,), (0,)), ((), ())), preferred_element_type=F32)


def factors(weights, keys, values, rates, scale):
    gate, upper, back = nt(weights[0], keys), nt(weights[1], keys), -nt(weights[2], values)
    sigma = jax.nn.sigmoid(gate)
    active = gate * sigma
    rates = rates * scale
    dgate = back * upper * sigma * (1.0 + gate * (1.0 - sigma))
    return (
        (rates[0:1] * dgate).astype(BF16),
        (rates[1:2] * (back * active)).astype(BF16),
        (-(rates[2:3] * (active * upper))).astype(BF16),
    )


def fill_factors(out, weights, keys, values, rates, scale, start):
    for at in range(0, keys.shape[0], TILE):
        part = factors(weights, keys[at : at + TILE], values[at : at + TILE], rates[:, at : at + TILE], scale)
        for i in range(3):
            out[i, :, start + at : start + at + TILE] = part[i]


def rescale(rows, target):
    return rows * (target / jnp.sqrt(jnp.sum(rows * rows, -1, keepdims=True) + 1e-06))


def norm(rows):
    return jnp.sqrt(jnp.sum(rows * rows, -1, keepdims=True))


def call(kernel, outs, args, scratch=(), specs=None, flops=0, limit=8):
    size = sum(a.size * a.dtype.itemsize for a in (*args, *outs))
    return pl.pallas_call(
        kernel,
        out_shape=list(outs),
        in_specs=specs or [VMEM] * len(args),
        out_specs=[VMEM] * len(outs),
        scratch_shapes=list(scratch),
        cost_estimate=pl.CostEstimate(flops=flops, bytes_accessed=size, transcendentals=0),
        compiler_params=pltpu.CompilerParams(vmem_limit_bytes=limit << 20),
    )(*args)


def shape(dims, dtype):
    return jax.ShapeDtypeStruct(dims, dtype)


def shards(queries, keys, values, rates, fast0):
    tokens, width = keys.shape
    hidden = fast0.shape[1]
    half, piece = hidden // 2, hidden // 16
    scale = (tokens * lax.axis_size("tok") * width) ** (-0.5)
    piece_bf, piece_f32 = shape((3, piece, width), BF16), shape((3, piece, width), F32)
    flops = 12 * tokens * width * half

    def swap(value):
        return lax.ppermute(value, "tok", [(t, t ^ 1) for t in range(16)])

    def to_peer(value, k):
        return lax.ppermute(value, "tok", [(t, t ^ (2 * k)) for t in range(16)])

    def along_block(value, k):
        return lax.ppermute(value, "block", [(b, b ^ k) for b in range(16)])

    def put_pieces(pieces, i, grad):
        for m in range(PEERS):
            p = -m % PEERS
            pieces[m][i] = grad[p * piece : (p + 1) * piece].astype(BF16)

    other_keys, other_values, other_rates = swap(keys), swap(values), swap(rates)

    def first(fast0_ref, keys_ref, values_ref, rates_ref, weights_ref, own_ref, total_ref, rows, left, sem):
        place = lax.axis_index("tok")
        chip, core = place // 2, place % 2
        copies = []
        for k in range(PEERS):
            begin = pl.multiple_of(core * half + (chip ^ PLACES[k]) * piece, piece)
            copies.append(pltpu.make_async_copy(fast0_ref.at[:, pl.ds(begin, piece)], rows.at[k], sem.at[k]))
            copies[-1].start()
        for k in range(PEERS):
            copies[k].wait()
            weights_ref[:, k * piece : (k + 1) * piece] = rows[k].astype(BF16)
        own_ref[...] = rows[0]
        weights = [weights_ref[i] for i in range(3)]
        fill_factors(left, weights, keys_ref, values_ref, rates_ref, scale, 0)
        for i in range(3):
            total_ref[i] = nn(left[i], (keys_ref if i < 2 else values_ref)[...])

    weights, own, total = call(
        first,
        [shape((3, half, width), BF16), piece_f32, shape((3, half, width), F32)],
        (pltpu.with_memory_space_constraint(fast0, pltpu.HBM), keys, values, rates),
        [pltpu.VMEM((PEERS, 3, piece, width), F32), pltpu.VMEM((3, half, tokens), BF16), pltpu.SemaphoreType.DMA((PEERS,))],
        [HBM, VMEM, VMEM, VMEM],
        flops,
        24,
    )

    def second(weights_ref, keys_ref, values_ref, rates_ref, total_ref, *rest):
        pieces, left = rest[:PEERS], rest[PEERS]
        weights = [weights_ref[i] for i in range(3)]
        fill_factors(left, weights, keys_ref, values_ref, rates_ref, scale, 0)
        for i in range(3):
            grad = total_ref[i] + nn(left[i], (keys_ref if i < 2 else values_ref)[...])
            put_pieces(pieces, i, grad)

    grads = call(
        second,
        [piece_bf] * PEERS,
        (weights, other_keys, other_values, other_rates, total),
        [pltpu.VMEM((3, half, tokens), BF16)],
        flops=flops,
        limit=24,
    )

    def scatter(pieces):
        return [pieces[0]] + [to_peer(pieces[m], PLACES[PEERS - m]) for m in range(1, PEERS)]

    def gather(value):
        return [value] + [to_peer(value, k) for k in PLACES[1:]]

    def summed(parts):
        total = parts[0][...].astype(F32)
        for part in parts[1:]:
            total = total + part[...].astype(F32)
        return total

    def update_one(own_ref, *rest):
        parts, (new_ref, new_bf_ref) = rest[:PEERS], rest[PEERS:]
        rows = own_ref[...]
        new = rescale(rows - summed(parts), norm(rows))
        new_ref[...] = new
        new_bf_ref[...] = new.astype(BF16)

    new, new_bf = call(update_one, [piece_f32, piece_bf], (own, *scatter(grads)))
    gathered = gather(new_bf)

    def again(*refs):
        shard_refs = refs[:PEERS]
        keys_ref, values_ref, rates_ref, keys2_ref, values2_ref, rates2_ref = refs[PEERS : PEERS + 6]
        pieces, left, weights_ref = refs[PEERS + 6 : 2 * PEERS + 6], refs[-2], refs[-1]
        for k in range(PEERS):
            weights_ref[:, k * piece : (k + 1) * piece] = shard_refs[k][...]
        weights = [weights_ref[i] for i in range(3)]
        fill_factors(left, weights, keys_ref, values_ref, rates_ref, scale, 0)
        fill_factors(left, weights, keys2_ref, values2_ref, rates2_ref, scale, tokens)
        for i in range(3):
            right = (keys_ref, keys2_ref) if i < 2 else (values_ref, values2_ref)
            grad = nn(left[i, :, :tokens], right[0][...]) + nn(left[i, :, tokens:], right[1][...])
            put_pieces(pieces, i, grad)

    grads = call(
        again,
        [piece_bf] * PEERS,
        (*gathered, keys, values, rates, other_keys, other_values, other_rates),
        [pltpu.VMEM((3, half, 2 * tokens), BF16), pltpu.VMEM((3, half, width), BF16)],
        flops=2 * flops,
        limit=24,
    )

    def update_two(own_ref, new_ref, *rest):
        parts, (change_ref, change_bf_ref) = rest[:PEERS], rest[PEERS:]
        rows = own_ref[...]
        change = rescale(new_ref[...] - summed(parts), norm(rows)) - rows
        change_ref[...] = change
        change_bf_ref[...] = change.astype(BF16)

    change, change_bf = call(update_two, [piece_f32, piece_bf], (own, new, *scatter(grads)))

    def near(change_ref, *rest):
        parts, (prefix_ref, ring_ref) = rest[:3], rest[3:]
        here = lax.axis_index("block") % 4
        prefix, ring = change_ref[...], change_ref[...]
        for k, ref in zip(RING, parts):
            part = ref[...].astype(F32)
            ring = ring + part
            prefix = prefix + jnp.where((here ^ k) < here, part, 0.0)
        prefix_ref[...] = prefix
        ring_ref[...] = ring.astype(BF16)

    prefix, ring = call(
        near, [piece_f32, piece_bf], (change, *[along_block(change_bf, k) for k in RING])
    )

    def far(own_ref, prefix_ref, *rest):
        parts, applied_ref = rest[:3], rest[3]
        here = lax.axis_index("block") // 4
        prefix, rows = prefix_ref[...], own_ref[...]
        for k, ref in zip(RING, parts):
            prefix = prefix + jnp.where((here ^ k) < here, ref[...].astype(F32), 0.0)
        applied_ref[...] = rescale(rows + prefix, norm(rows)).astype(BF16)

    (applied,) = call(far, [piece_bf], (own, prefix, *[along_block(ring, 4 * k) for k in RING]))

    mine = gather(applied)
    theirs = [swap(part) for part in mine]

    def apply_half(queries, part_refs):
        rows = [jnp.concatenate([ref[i] for ref in part_refs], 0) for i in range(3)]
        gate, upper = nt(queries, rows[0]), nt(queries, rows[1])
        return nn((jax.nn.silu(gate) * upper).astype(BF16), rows[2])

    def apply_mine(queries_ref, *rest):
        for at in range(0, tokens, TILE):
            rest[-1][at : at + TILE] = apply_half(queries_ref[at : at + TILE], rest[:-1])

    def apply_theirs(queries_ref, partial_ref, *rest):
        for at in range(0, tokens, TILE):
            rows = slice(at, at + TILE)
            rest[-1][rows] = (partial_ref[rows] + apply_half(queries_ref[rows], rest[:-1])).astype(BF16)

    (partial,) = call(apply_mine, [shape((tokens, width), F32)], (queries, *mine), flops=flops // 2, limit=24)
    (outputs,) = call(apply_theirs, [shape((tokens, width), BF16)], (queries, partial, *theirs), flops=flops // 2, limit=24)
    return outputs


def solution(mesh):
    return jax.shard_map(
        shards,
        mesh=mesh,
        in_specs=(
            P(("block", "tok"), None),
            P(("block", "tok"), None),
            P(("block", "tok"), None),
            P(None, ("block", "tok")),
            P(),
        ),
        out_specs=P(("block", "tok"), None),
        check_vma=False,
    )
```

```python
import jax
import jax.numpy as jnp
from jax import lax
from jax.experimental import pallas as pl
from jax.experimental.pallas import tpu as pltpu
from jax.sharding import PartitionSpec as P

F32, BF16 = jnp.float32, jnp.bfloat16
VMEM = pl.BlockSpec(memory_space=pltpu.VMEM)
HBM = pl.BlockSpec(memory_space=pltpu.HBM)
TILE = 512
PEERS = 8
RING = (1, 3, 2)
PLACES = (0, 1, 4, 7, 3, 5, 2, 6)
SENDS = (6, 2, 7, 4, 1, 3, 5, 0)
LOADS = PEERS + 2


def nt(a, b):
    return lax.dot_general(a, b, (((1,), (1,)), ((), ())), preferred_element_type=F32)


def nn(a, b):
    return lax.dot_general(a, b, (((1,), (0,)), ((), ())), preferred_element_type=F32)


def factors(weights, keys, values, rates, scale):
    gate, upper, back = nt(weights[0], keys), nt(weights[1], keys), -nt(weights[2], values)
    sigma = jax.nn.sigmoid(gate)
    active = gate * sigma
    rates = rates * scale
    dgate = back * upper * sigma * (1.0 + gate * (1.0 - sigma))
    return (
        (rates[0:1] * dgate).astype(BF16),
        (rates[1:2] * (back * active)).astype(BF16),
        (-(rates[2:3] * (active * upper))).astype(BF16),
    )


def fill_factors(out, weights, keys, values, rates, scale, start):
    for at in range(0, keys.shape[0], TILE):
        part = factors(weights, keys[at : at + TILE], values[at : at + TILE], rates[:, at : at + TILE], scale)
        for i in range(3):
            out[i, :, start + at : start + at + TILE] = part[i]


def rescale(rows, target):
    return rows * (target / jnp.sqrt(jnp.sum(rows * rows, -1, keepdims=True) + 1e-06))


def norm(rows):
    return jnp.sqrt(jnp.sum(rows * rows, -1, keepdims=True))


def call(kernel, outs, args, scratch=(), specs=None, flops=0, limit=8):
    size = sum(a.size * a.dtype.itemsize for a in (*args, *outs))
    return pl.pallas_call(
        kernel,
        out_shape=list(outs),
        in_specs=specs or [VMEM] * len(args),
        out_specs=[VMEM] * len(outs),
        scratch_shapes=list(scratch),
        cost_estimate=pl.CostEstimate(flops=flops, bytes_accessed=size, transcendentals=0),
        compiler_params=pltpu.CompilerParams(vmem_limit_bytes=limit << 20),
    )(*args)


def shape(dims, dtype):
    return jax.ShapeDtypeStruct(dims, dtype)


def shards(queries, keys, values, rates, fast0):
    tokens, width = keys.shape
    hidden = fast0.shape[1]
    half, piece = hidden // 2, hidden // 16
    scale = (tokens * lax.axis_size("tok") * width) ** (-0.5)
    piece_bf, piece_f32 = shape((3, piece, width), BF16), shape((3, piece, width), F32)
    flops = 12 * tokens * width * half

    def swap(value):
        return lax.ppermute(value, "tok", [(t, t ^ 1) for t in range(16)])

    def to_peer(value, k):
        return lax.ppermute(value, "tok", [(t, t ^ (2 * k)) for t in range(16)])

    def along_block(value, k):
        return lax.ppermute(value, "block", [(b, b ^ k) for b in range(16)])

    def put_pieces(pieces, i, grad):
        for m, k in enumerate(SENDS):
            p = PLACES.index(k)
            pieces[m][i] = grad[p * piece : (p + 1) * piece].astype(BF16)

    other_keys, other_values, other_rates = swap(keys), swap(values), swap(rates)

    def in_hbm(value):
        return pltpu.with_memory_space_constraint(value, pltpu.HBM)

    def first(fast0_ref, keys_hbm, values_hbm, rates_ref, weights_ref, own_ref, total_ref, rows, keys_ref, values_ref, left, sem):
        place = lax.axis_index("tok")
        chip, core = place // 2, place % 2
        copies = []

        def load(source, target):
            copies.append(pltpu.make_async_copy(source, target, sem.at[len(copies)]))
            copies[-1].start()

        for p in range(PEERS):
            begin = pl.multiple_of(core * half + (chip ^ PLACES[p]) * piece, piece)
            load(fast0_ref.at[:, pl.ds(begin, piece)], rows.at[p])
        load(keys_hbm, keys_ref)
        load(values_hbm, values_ref)
        for p in range(PEERS):
            copies[p].wait()
            weights_ref[:, p * piece : (p + 1) * piece] = rows[p].astype(BF16)
        own_ref[...] = rows[0]
        weights = [weights_ref[i] for i in range(3)]
        copies[PEERS].wait()
        copies[PEERS + 1].wait()
        fill_factors(left, weights, keys_ref, values_ref, rates_ref, scale, 0)
        for i in range(3):
            total_ref[i] = nn(left[i], (keys_ref if i < 2 else values_ref)[...])

    weights, own, total = call(
        first,
        [shape((3, half, width), BF16), piece_f32, shape((3, half, width), F32)],
        (in_hbm(fast0), in_hbm(keys), in_hbm(values), rates),
        [
            pltpu.VMEM((PEERS, 3, piece, width), F32),
            pltpu.VMEM((tokens, width), BF16),
            pltpu.VMEM((tokens, width), BF16),
            pltpu.VMEM((3, half, tokens), BF16),
            pltpu.SemaphoreType.DMA((LOADS,)),
        ],
        [HBM, HBM, HBM, VMEM],
        flops,
        24,
    )

    def second(weights_ref, keys_ref, values_ref, rates_ref, total_ref, *rest):
        pieces, left = rest[:PEERS], rest[PEERS]
        weights = [weights_ref[i] for i in range(3)]
        fill_factors(left, weights, keys_ref, values_ref, rates_ref, scale, 0)
        for i in range(3):
            grad = total_ref[i] + nn(left[i], (keys_ref if i < 2 else values_ref)[...])
            put_pieces(pieces, i, grad)

    grads = call(
        second,
        [piece_bf] * PEERS,
        (weights, other_keys, other_values, other_rates, total),
        [pltpu.VMEM((3, half, tokens), BF16)],
        flops=flops,
        limit=24,
    )

    def merge(a_ref, b_ref, out_ref):
        out_ref[...] = (a_ref[...].astype(F32) + b_ref[...].astype(F32)).astype(BF16)

    def scatter(pieces):
        send = dict(zip(SENDS, pieces))
        far, cross = to_peer(send[6], 3), to_peer(send[2], 1)
        terms = [to_peer(send[k], k) for k in (7, 4, 1)]
        for k, relayed in ((5, far), (3, cross)):
            terms.append(to_peer(call(merge, [piece_bf], (send[k], relayed))[0], k))
        return [send[0]] + terms

    def gather(value):
        found = {k: to_peer(value, k) for k in (1, 4, 7, 3, 5)}
        found[0], found[2], found[6] = value, to_peer(found[3], 1), to_peer(found[5], 3)
        return [found[k] for k in PLACES]

    def summed(parts):
        total = parts[0][...].astype(F32)
        for part in parts[1:]:
            total = total + part[...].astype(F32)
        return total

    def update_one(own_ref, *rest):
        parts, (new_ref, new_bf_ref) = rest[:-2], rest[-2:]
        rows = own_ref[...]
        new = rescale(rows - summed(parts), norm(rows))
        new_ref[...] = new
        new_bf_ref[...] = new.astype(BF16)

    new, new_bf = call(update_one, [piece_f32, piece_bf], (own, *scatter(grads)))
    gathered = gather(new_bf)

    def again(*refs):
        shard_refs = refs[:PEERS]
        keys_ref, values_ref, rates_ref, keys2_ref, values2_ref, rates2_ref = refs[PEERS : PEERS + 6]
        pieces, left, weights_ref = refs[PEERS + 6 : 2 * PEERS + 6], refs[-2], refs[-1]
        for k in range(PEERS):
            weights_ref[:, k * piece : (k + 1) * piece] = shard_refs[k][...]
        weights = [weights_ref[i] for i in range(3)]
        fill_factors(left, weights, keys_ref, values_ref, rates_ref, scale, 0)
        fill_factors(left, weights, keys2_ref, values2_ref, rates2_ref, scale, tokens)
        for i in range(3):
            right = (keys_ref, keys2_ref) if i < 2 else (values_ref, values2_ref)
            grad = nn(left[i, :, :tokens], right[0][...]) + nn(left[i, :, tokens:], right[1][...])
            put_pieces(pieces, i, grad)

    grads = call(
        again,
        [piece_bf] * PEERS,
        (*gathered, keys, values, rates, other_keys, other_values, other_rates),
        [pltpu.VMEM((3, half, 2 * tokens), BF16), pltpu.VMEM((3, half, width), BF16)],
        flops=2 * flops,
        limit=24,
    )

    def update_two(own_ref, new_ref, *rest):
        parts, (change_ref, change_bf_ref) = rest[:-2], rest[-2:]
        rows = own_ref[...]
        change = rescale(new_ref[...] - summed(parts), norm(rows)) - rows
        change_ref[...] = change
        change_bf_ref[...] = change.astype(BF16)

    change, change_bf = call(update_two, [piece_f32, piece_bf], (own, new, *scatter(grads)))

    def near(change_ref, *rest):
        parts, (prefix_ref, ring_ref) = rest[:3], rest[3:]
        here = lax.axis_index("block") % 4
        prefix, ring = change_ref[...], change_ref[...]
        for k, ref in zip(RING, parts):
            part = ref[...].astype(F32)
            ring = ring + part
            prefix = prefix + jnp.where((here ^ k) < here, part, 0.0)
        prefix_ref[...] = prefix
        ring_ref[...] = ring.astype(BF16)

    prefix, ring = call(
        near, [piece_f32, piece_bf], (change, *[along_block(change_bf, k) for k in RING])
    )

    def far(own_ref, prefix_ref, *rest):
        parts, applied_ref = rest[:3], rest[3]
        here = lax.axis_index("block") // 4
        prefix, rows = prefix_ref[...], own_ref[...]
        for k, ref in zip(RING, parts):
            prefix = prefix + jnp.where((here ^ k) < here, ref[...].astype(F32), 0.0)
        applied_ref[...] = rescale(rows + prefix, norm(rows)).astype(BF16)

    (applied,) = call(far, [piece_bf], (own, prefix, *[along_block(ring, 4 * k) for k in RING]))

    mine = gather(applied)
    theirs = [swap(part) for part in mine]

    def apply_half(queries, part_refs):
        rows = [jnp.concatenate([ref[i] for ref in part_refs], 0) for i in range(3)]
        gate, upper = nt(queries, rows[0]), nt(queries, rows[1])
        return nn((jax.nn.silu(gate) * upper).astype(BF16), rows[2])

    def apply_mine(queries_ref, *rest):
        for at in range(0, tokens, TILE):
            rest[-1][at : at + TILE] = apply_half(queries_ref[at : at + TILE], rest[:-1])

    def apply_theirs(queries_ref, partial_ref, *rest):
        for at in range(0, tokens, TILE):
            rows = slice(at, at + TILE)
            rest[-1][rows] = (partial_ref[rows] + apply_half(queries_ref[rows], rest[:-1])).astype(BF16)

    (partial,) = call(apply_mine, [shape((tokens, width), F32)], (queries, *mine), flops=flops // 2, limit=24)
    (outputs,) = call(apply_theirs, [shape((tokens, width), BF16)], (queries, partial, *theirs), flops=flops // 2, limit=24)
    return outputs


def solution(mesh):
    return jax.shard_map(
        shards,
        mesh=mesh,
        in_specs=(
            P(("block", "tok"), None),
            P(("block", "tok"), None),
            P(("block", "tok"), None),
            P(None, ("block", "tok")),
            P(),
        ),
        out_specs=P(("block", "tok"), None),
        check_vma=False,
    )
```

```python
import jax
import jax.numpy as jnp
from jax import lax
from jax.experimental import pallas as pl
from jax.experimental.pallas import tpu as pltpu
from jax.sharding import PartitionSpec as P

F32, BF16 = jnp.float32, jnp.bfloat16
VMEM = pl.BlockSpec(memory_space=pltpu.VMEM)
HBM = pl.BlockSpec(memory_space=pltpu.HBM)
TILE = 512
PEERS = 8
RING = (1, 3, 2)
PLACES = (0, 1, 4, 3, 5, 7, 2, 6)
RELAYS = ((6, 3, 5), (2, 1, 3), (7, 4, 3))
TURNS = ((0, 1, 2, 3, 4, 5, 6, 7), (0, 3, 7, 4, 1, 2, 6, 5))
RING_TURNS = ((0, 1, 2, 3), (0, 3, 2, 1))
SENDS = (6, 2, 7, 4, 1, 5, 3, 0)


def nt(a, b):
    return lax.dot_general(a, b, (((1,), (1,)), ((), ())), preferred_element_type=F32)


def nn(a, b):
    return lax.dot_general(a, b, (((1,), (0,)), ((), ())), preferred_element_type=F32)


def factors(weights, keys, values, rates, scale):
    gate, upper, back = nt(weights[0], keys), nt(weights[1], keys), -nt(weights[2], values)
    sigma = jax.nn.sigmoid(gate)
    active = gate * sigma
    rates = rates * scale
    dgate = back * upper * sigma * (1.0 + gate * (1.0 - sigma))
    return (
        (rates[0:1] * dgate).astype(BF16),
        (rates[1:2] * (back * active)).astype(BF16),
        (-(rates[2:3] * (active * upper))).astype(BF16),
    )


def fill_factors(out, weights, keys, values, rates, scale, start):
    for at in range(0, keys.shape[0], TILE):
        part = factors(weights, keys[at : at + TILE], values[at : at + TILE], rates[:, at : at + TILE], scale)
        for i in range(3):
            out[i, :, start + at : start + at + TILE] = part[i]


def rescale(rows, target):
    return rows * (target / jnp.sqrt(jnp.sum(rows * rows, -1, keepdims=True) + 1e-06))


def norm(rows):
    return jnp.sqrt(jnp.sum(rows * rows, -1, keepdims=True))


def call(kernel, outs, args, scratch=(), specs=None, flops=0, limit=8, out_specs=None):
    size = sum(a.size * a.dtype.itemsize for a in (*args, *outs))
    return pl.pallas_call(
        kernel,
        out_shape=list(outs),
        in_specs=specs or [VMEM] * len(args),
        out_specs=out_specs or [VMEM] * len(outs),
        scratch_shapes=list(scratch),
        cost_estimate=pl.CostEstimate(flops=flops, bytes_accessed=size, transcendentals=0),
        compiler_params=pltpu.CompilerParams(vmem_limit_bytes=limit << 20),
    )(*args)


def shape(dims, dtype):
    return jax.ShapeDtypeStruct(dims, dtype)


def shards(queries, keys, values, rates, fast0):
    tokens, width = keys.shape
    hidden = fast0.shape[1]
    half, piece = hidden // 2, hidden // 16
    scale = (tokens * lax.axis_size("tok") * width) ** (-0.5)
    piece_bf, piece_f32 = shape((3, piece, width), BF16), shape((3, piece, width), F32)
    flops = 12 * tokens * width * half

    def swap(value):
        return lax.ppermute(value, "tok", [(t, t ^ 1) for t in range(16)])

    def to_peer(value, k):
        return lax.ppermute(value, "tok", [(t, t ^ (2 * TURNS[t % 2][k])) for t in range(16)])

    def along_block(value, k, step):
        pairs = [
            (16 * b + t, 16 * (b ^ (step * RING_TURNS[t % 2][k])) + t) for b in range(16) for t in range(16)
        ]
        return lax.ppermute(value, ("block", "tok"), pairs)

    def before(here, k):
        core = lax.axis_index("tok") % 2
        return (here ^ jnp.where(core == 0, RING_TURNS[0][k], RING_TURNS[1][k])) < here

    def put_pieces(pieces, i, grad):
        for m, k in enumerate(SENDS):
            p = PLACES.index(k)
            pieces[m][i] = grad[p * piece : (p + 1) * piece].astype(BF16)

    other_keys, other_values, other_rates = swap(keys), swap(values), swap(rates)

    def in_hbm(value):
        return pltpu.with_memory_space_constraint(value, pltpu.HBM)

    def first(fast0_ref, keys_hbm, values_hbm, rates_hbm, weights_ref, own_ref, total_ref, rows, keys_ref, values_ref, rates_ref, left, sem):
        place = lax.axis_index("tok")
        chip, core = place // 2, place % 2
        copies = []

        def load(source, target):
            copies.append(pltpu.make_async_copy(source, target, sem.at[len(copies)]))
            copies[-1].start()

        for p in range(PEERS):
            k = jnp.where(core == 0, TURNS[0][PLACES[p]], TURNS[1][PLACES[p]])
            begin = pl.multiple_of(core * half + (chip ^ k) * piece, piece)
            load(fast0_ref.at[:, pl.ds(begin, piece)], rows.at[p])
        load(rates_hbm, rates_ref)
        for at in range(0, tokens, TILE):
            load(keys_hbm.at[at : at + TILE], keys_ref.at[at : at + TILE])
            load(values_hbm.at[at : at + TILE], values_ref.at[at : at + TILE])
        for p in range(PEERS):
            copies[p].wait()
            weights_ref[:, p * piece : (p + 1) * piece] = rows[p].astype(BF16)
        own_ref[...] = rows[0]
        weights = [weights_ref[i] for i in range(3)]
        copies[PEERS].wait()
        for n, at in enumerate(range(0, tokens, TILE)):
            copies[PEERS + 1 + 2 * n].wait()
            copies[PEERS + 2 + 2 * n].wait()
            tile = slice(at, at + TILE)
            fill_factors(left, weights, keys_ref[tile], values_ref[tile], rates_ref[:, tile], scale, at)
        for i in range(3):
            total_ref[i] = nn(left[i], (keys_ref if i < 2 else values_ref)[...])

    weights, own, total = call(
        first,
        [shape((3, half, width), BF16), piece_f32, shape((3, half, width), F32)],
        (in_hbm(fast0), in_hbm(keys), in_hbm(values), in_hbm(rates)),
        [
            pltpu.VMEM((PEERS, 3, piece, width), F32),
            pltpu.VMEM((tokens, width), BF16),
            pltpu.VMEM((tokens, width), BF16),
            pltpu.VMEM((3, tokens), F32),
            pltpu.VMEM((3, half, tokens), BF16),
            pltpu.SemaphoreType.DMA((PEERS + 1 + 2 * (tokens // TILE),)),
        ],
        [HBM] * 4,
        flops,
        24,
    )

    def second(weights_ref, keys_ref, values_ref, rates_ref, total_ref, *rest):
        pieces, left = rest[:PEERS], rest[PEERS]
        weights = [weights_ref[i] for i in range(3)]
        fill_factors(left, weights, keys_ref, values_ref, rates_ref, scale, 0)
        for i in range(3):
            grad = total_ref[i] + nn(left[i], (keys_ref if i < 2 else values_ref)[...])
            put_pieces(pieces, i, grad)

    grads = call(
        second,
        [piece_bf] * PEERS,
        (weights, other_keys, other_values, other_rates, total),
        [pltpu.VMEM((3, half, tokens), BF16)],
        flops=flops,
        limit=24,
    )

    def merge(*refs):
        refs[-1][...] = summed(refs[:-1]).astype(BF16)

    def scatter(pieces):
        send = dict(zip(SENDS, pieces))
        relayed = {k: to_peer(send[k], way) for k, way, _ in RELAYS}
        for k, _, onward in RELAYS:
            send[onward] = (send[onward] if isinstance(send[onward], tuple) else (send[onward],)) + (relayed[k],)
        terms = [to_peer(send[k], k) for k in (4, 1)]
        for k in (5, 3):
            terms.append(to_peer(call(merge, [piece_bf], send[k])[0], k))
        return [send[0]] + terms

    def gather(value):
        found = {k: to_peer(value, k) for k in (1, 4, 3, 5)}
        found[0] = value
        for k, way, onward in RELAYS:
            found[k] = to_peer(found[onward], way)
        return [found[k] for k in PLACES]

    def summed(parts):
        total = parts[0][...].astype(F32)
        for part in parts[1:]:
            total = total + part[...].astype(F32)
        return total

    def update_one(own_ref, *rest):
        parts, (new_ref, new_bf_ref) = rest[:-2], rest[-2:]
        rows = own_ref[...]
        new = rescale(rows - summed(parts), norm(rows))
        new_ref[...] = new
        new_bf_ref[...] = new.astype(BF16)

    new, new_bf = call(update_one, [piece_f32, piece_bf], (own, *scatter(grads)))
    gathered = gather(new_bf)

    def again(*refs):
        shard_refs = refs[:PEERS]
        keys_ref, values_ref, rates_ref, keys2_ref, values2_ref, rates2_ref = refs[PEERS : PEERS + 6]
        pieces, left, weights_ref = refs[PEERS + 6 : 2 * PEERS + 6], refs[-2], refs[-1]
        for k in range(PEERS):
            weights_ref[:, k * piece : (k + 1) * piece] = shard_refs[k][...]
        weights = [weights_ref[i] for i in range(3)]
        fill_factors(left, weights, keys_ref, values_ref, rates_ref, scale, 0)
        fill_factors(left, weights, keys2_ref, values2_ref, rates2_ref, scale, tokens)
        for i in range(3):
            right = (keys_ref, keys2_ref) if i < 2 else (values_ref, values2_ref)
            grad = nn(left[i, :, :tokens], right[0][...]) + nn(left[i, :, tokens:], right[1][...])
            put_pieces(pieces, i, grad)

    grads = call(
        again,
        [piece_bf] * PEERS,
        (*gathered, keys, values, rates, other_keys, other_values, other_rates),
        [pltpu.VMEM((3, half, 2 * tokens), BF16), pltpu.VMEM((3, half, width), BF16)],
        flops=2 * flops,
        limit=24,
    )

    def update_two(own_ref, new_ref, *rest):
        parts, (change_ref, change_bf_ref) = rest[:-2], rest[-2:]
        rows = own_ref[...]
        change = rescale(new_ref[...] - summed(parts), norm(rows)) - rows
        change_ref[...] = change
        change_bf_ref[...] = change.astype(BF16)

    change, change_bf = call(update_two, [piece_f32, piece_bf], (own, new, *scatter(grads)))

    def near(change_ref, *rest):
        parts, (prefix_ref, ring_ref) = rest[:3], rest[3:]
        here = lax.axis_index("block") % 4
        prefix, ring = change_ref[...], change_ref[...]
        for k, ref in zip(RING, parts):
            part = ref[...].astype(F32)
            ring = ring + part
            prefix = prefix + jnp.where(before(here, k), part, 0.0)
        prefix_ref[...] = prefix
        ring_ref[...] = ring.astype(BF16)

    prefix, ring = call(
        near, [piece_f32, piece_bf], (change, *[along_block(change_bf, k, 1) for k in RING])
    )

    def far(own_ref, prefix_ref, *rest):
        parts, applied_ref = rest[:3], rest[3]
        here = lax.axis_index("block") // 4
        prefix, rows = prefix_ref[...], own_ref[...]
        for k, ref in zip(RING, parts):
            prefix = prefix + jnp.where(before(here, k), ref[...].astype(F32), 0.0)
        applied_ref[...] = rescale(rows + prefix, norm(rows)).astype(BF16)

    (applied,) = call(far, [piece_bf], (own, prefix, *[along_block(ring, k, 4) for k in RING]))

    mine = gather(applied)
    theirs = [swap(part) for part in mine]

    def apply_to(queries, weights):
        gate, upper = nt(queries, weights[0]), nt(queries, weights[1])
        return nn((jax.nn.silu(gate) * upper).astype(BF16), weights[2])

    def joined(part_refs):
        return [jnp.concatenate([ref[i] for ref in part_refs], 0) for i in range(3)]

    def apply_mine(queries_ref, *rest):
        weights = joined(rest[:-1])
        for at in range(0, tokens, TILE):
            rest[-1][at : at + TILE] = apply_to(queries_ref[at : at + TILE], weights)

    def apply_theirs(queries_ref, partial_ref, *rest):
        part_refs, (out_hbm, out_ref, sem) = rest[:-3], rest[-3:]
        weights = joined(part_refs)
        copies = []
        for n, at in enumerate(range(0, tokens, TILE)):
            tile = slice(at, at + TILE)
            out_ref[tile] = (partial_ref[tile] + apply_to(queries_ref[tile], weights)).astype(BF16)
            copies.append(pltpu.make_async_copy(out_ref.at[tile], out_hbm.at[tile], sem.at[n]))
            copies[-1].start()
        for copy in copies:
            copy.wait()

    (partial,) = call(apply_mine, [shape((tokens, width), F32)], (queries, *mine), flops=flops // 2, limit=24)
    (outputs,) = call(
        apply_theirs,
        [shape((tokens, width), BF16)],
        (queries, partial, *theirs),
        [pltpu.VMEM((tokens, width), BF16), pltpu.SemaphoreType.DMA((tokens // TILE,))],
        flops=flops // 2,
        limit=24,
        out_specs=[HBM],
    )
    return outputs


def solution(mesh):
    return jax.shard_map(
        shards,
        mesh=mesh,
        in_specs=(
            P(("block", "tok"), None),
            P(("block", "tok"), None),
            P(("block", "tok"), None),
            P(None, ("block", "tok")),
            P(),
        ),
        out_specs=P(("block", "tok"), None),
        check_vma=False,
    )
```

```python
import jax
import jax.numpy as jnp
from jax import lax
from jax.experimental import pallas as pl
from jax.experimental.pallas import tpu as pltpu
from jax.sharding import PartitionSpec as P

F32, BF16 = jnp.float32, jnp.bfloat16
VMEM = pl.BlockSpec(memory_space=pltpu.VMEM)
HBM = pl.BlockSpec(memory_space=pltpu.HBM)
TILE = 512
PEERS = 8
RING = (1, 3, 2)
PLACES = (0, 1, 4, 3, 5, 7, 2, 6)
RELAYS = ((6, 3, 5), (2, 1, 3), (7, 4, 3))
TURNS = ((0, 1, 2, 3, 4, 5, 6, 7), (0, 3, 7, 4, 1, 2, 6, 5))
SUM_TURNS = (TURNS[1], TURNS[0])
RING_TURNS = ((0, 1, 2, 3), (0, 3, 2, 1))
SENDS = (6, 2, 7, 4, 1, 5, 3, 0)


def nt(a, b):
    return lax.dot_general(a, b, (((1,), (1,)), ((), ())), preferred_element_type=F32)


def nn(a, b):
    return lax.dot_general(a, b, (((1,), (0,)), ((), ())), preferred_element_type=F32)


def factors(weights, keys, values, rates, scale):
    gate, upper, back = nt(weights[0], keys), nt(weights[1], keys), -nt(weights[2], values)
    sigma = jax.nn.sigmoid(gate)
    active = gate * sigma
    rates = rates * scale
    dgate = back * upper * sigma * (1.0 + gate * (1.0 - sigma))
    return (
        (rates[0:1] * dgate).astype(BF16),
        (rates[1:2] * (back * active)).astype(BF16),
        (-(rates[2:3] * (active * upper))).astype(BF16),
    )


def fill_factors(out, weights, keys, values, rates, scale, start):
    for at in range(0, keys.shape[0], TILE):
        part = factors(weights, keys[at : at + TILE], values[at : at + TILE], rates[:, at : at + TILE], scale)
        for i in range(3):
            out[i, :, start + at : start + at + part[i].shape[1]] = part[i]


def rescale(rows, target):
    return rows * (target / jnp.sqrt(jnp.sum(rows * rows, -1, keepdims=True) + 1e-06))


def norm(rows):
    return jnp.sqrt(jnp.sum(rows * rows, -1, keepdims=True))


def call(kernel, outs, args, scratch=(), specs=None, flops=0, limit=8, out_specs=None):
    size = sum(a.size * a.dtype.itemsize for a in (*args, *outs))
    return pl.pallas_call(
        kernel,
        out_shape=list(outs),
        in_specs=specs or [VMEM] * len(args),
        out_specs=out_specs or [VMEM] * len(outs),
        scratch_shapes=list(scratch),
        cost_estimate=pl.CostEstimate(flops=flops, bytes_accessed=size, transcendentals=0),
        compiler_params=pltpu.CompilerParams(vmem_limit_bytes=limit << 20),
    )(*args)


def shape(dims, dtype):
    return jax.ShapeDtypeStruct(dims, dtype)


def shards(queries, keys, values, rates, fast0):
    tokens, width = keys.shape
    hidden = fast0.shape[1]
    half, piece = hidden // 2, hidden // 16
    scale = (tokens * lax.axis_size("tok") * width) ** (-0.5)
    piece_bf, piece_f32 = shape((3, piece, width), BF16), shape((3, piece, width), F32)
    flops = 12 * tokens * width * half

    def swap(value):
        return lax.ppermute(value, "tok", [(t, t ^ 1) for t in range(16)])

    def to_peer(value, k, turns=TURNS):
        return lax.ppermute(value, "tok", [(t, t ^ (2 * turns[t % 2][k])) for t in range(16)])

    def along_block(value, k, step):
        pairs = [
            (16 * b + t, 16 * (b ^ (step * RING_TURNS[t % 2][k])) + t) for b in range(16) for t in range(16)
        ]
        return lax.ppermute(value, ("block", "tok"), pairs)

    def before(here, k):
        core = lax.axis_index("tok") % 2
        return (here ^ jnp.where(core == 0, RING_TURNS[0][k], RING_TURNS[1][k])) < here

    def put_pieces(pieces, i, grad, grad_ref):
        grad_ref[...] = grad
        for m, k in enumerate(SENDS):
            at = [[TURNS[c][place] for place in PLACES].index(SUM_TURNS[c][k]) * piece for c in range(2)]
            begin = pl.multiple_of(jnp.where(lax.axis_index("tok") % 2 == 0, at[0], at[1]), piece)
            pieces[m][i] = grad_ref[pl.ds(begin, piece)].astype(BF16)

    other_keys, other_values, other_rates = swap(keys), swap(values), swap(rates)

    def in_hbm(value):
        return pltpu.with_memory_space_constraint(value, pltpu.HBM)

    def first(fast0_ref, keys_hbm, values_hbm, rates_hbm, weights_ref, own_ref, total_ref, rows, keys_ref, values_ref, rates_ref, left, sem):
        place = lax.axis_index("tok")
        chip, core = place // 2, place % 2
        copies = []

        def load(source, target):
            copies.append(pltpu.make_async_copy(source, target, sem.at[len(copies)]))
            copies[-1].start()

        for p in range(PEERS):
            k = jnp.where(core == 0, TURNS[0][PLACES[p]], TURNS[1][PLACES[p]])
            begin = pl.multiple_of(core * half + (chip ^ k) * piece, piece)
            load(fast0_ref.at[:, pl.ds(begin, piece)], rows.at[p])
        load(rates_hbm, rates_ref)
        for at in range(0, tokens, TILE // 2):
            load(keys_hbm.at[at : at + TILE // 2], keys_ref.at[at : at + TILE // 2])
            load(values_hbm.at[at : at + TILE // 2], values_ref.at[at : at + TILE // 2])
        for p in range(PEERS):
            copies[p].wait()
            weights_ref[:, p * piece : (p + 1) * piece] = rows[p].astype(BF16)
        own_ref[...] = rows[0]
        weights = [weights_ref[i] for i in range(3)]
        copies[PEERS].wait()
        for n, at in enumerate(range(0, tokens, TILE // 2)):
            copies[PEERS + 1 + 2 * n].wait()
            copies[PEERS + 2 + 2 * n].wait()
            tile = slice(at, at + TILE // 2)
            fill_factors(left, weights, keys_ref[tile], values_ref[tile], rates_ref[:, tile], scale, at)
        for i in range(3):
            total_ref[i] = nn(left[i], (keys_ref if i < 2 else values_ref)[...])

    weights, own, total = call(
        first,
        [shape((3, half, width), BF16), piece_f32, shape((3, half, width), F32)],
        (in_hbm(fast0), in_hbm(keys), in_hbm(values), in_hbm(rates)),
        [
            pltpu.VMEM((PEERS, 3, piece, width), F32),
            pltpu.VMEM((tokens, width), BF16),
            pltpu.VMEM((tokens, width), BF16),
            pltpu.VMEM((3, tokens), F32),
            pltpu.VMEM((3, half, tokens), BF16),
            pltpu.SemaphoreType.DMA((PEERS + 1 + 4 * (tokens // TILE),)),
        ],
        [HBM] * 4,
        flops,
        24,
    )

    def second(weights_ref, keys_ref, values_ref, rates_ref, total_ref, *rest):
        pieces, left, grad_ref = rest[:-2], rest[-2], rest[-1]
        weights = [weights_ref[i] for i in range(3)]
        fill_factors(left, weights, keys_ref, values_ref, rates_ref, scale, 0)
        for i in range(3):
            grad = total_ref[i] + nn(left[i], (keys_ref if i < 2 else values_ref)[...])
            put_pieces(pieces, i, grad, grad_ref)

    grads = call(
        second,
        [piece_bf] * PEERS,
        (weights, other_keys, other_values, other_rates, total),
        [pltpu.VMEM((3, half, tokens), BF16), pltpu.VMEM((half, width), F32)],
        flops=flops,
        limit=24,
    )

    def merge(*refs):
        refs[-1][...] = summed(refs[:-1]).astype(BF16)

    def scatter(pieces):
        send = dict(zip(SENDS, pieces))
        relayed = {k: to_peer(send[k], way, SUM_TURNS) for k, way, _ in RELAYS}
        for k, _, onward in RELAYS:
            send[onward] = (send[onward] if isinstance(send[onward], tuple) else (send[onward],)) + (relayed[k],)
        terms = [to_peer(send[k], k, SUM_TURNS) for k in (4, 1)]
        for k in (5, 3):
            terms.append(to_peer(call(merge, [piece_bf], send[k])[0], k, SUM_TURNS))
        return [send[0]] + terms

    def gather(value):
        found = {k: to_peer(value, k) for k in (1, 4, 3, 5)}
        found[0] = value
        for k, way, onward in RELAYS:
            found[k] = to_peer(found[onward], way)
        return [found[k] for k in PLACES]

    def summed(parts):
        total = parts[0][...].astype(F32)
        for part in parts[1:]:
            total = total + part[...].astype(F32)
        return total

    def update_one(own_ref, *rest):
        parts, (new_ref, new_bf_ref) = rest[:-2], rest[-2:]
        rows = own_ref[...]
        new = rescale(rows - summed(parts), norm(rows))
        new_ref[...] = new
        new_bf_ref[...] = new.astype(BF16)

    new, new_bf = call(update_one, [piece_f32, piece_bf], (own, *scatter(grads)))
    gathered = gather(new_bf)

    def again(*refs):
        shard_refs = refs[:PEERS]
        keys_ref, values_ref, rates_ref, keys2_ref, values2_ref, rates2_ref = refs[PEERS : PEERS + 6]
        pieces, left, weights_ref, grad_ref = refs[PEERS + 6 : -3], refs[-3], refs[-2], refs[-1]
        for k in range(PEERS):
            weights_ref[:, k * piece : (k + 1) * piece] = shard_refs[k][...]
        weights = [weights_ref[i] for i in range(3)]
        fill_factors(left, weights, keys_ref, values_ref, rates_ref, scale, 0)
        fill_factors(left, weights, keys2_ref, values2_ref, rates2_ref, scale, tokens)
        for i in range(3):
            right = (keys_ref, keys2_ref) if i < 2 else (values_ref, values2_ref)
            grad = nn(left[i, :, :tokens], right[0][...]) + nn(left[i, :, tokens:], right[1][...])
            put_pieces(pieces, i, grad, grad_ref)

    grads = call(
        again,
        [piece_bf] * PEERS,
        (*gathered, keys, values, rates, other_keys, other_values, other_rates),
        [pltpu.VMEM((3, half, 2 * tokens), BF16), pltpu.VMEM((3, half, width), BF16), pltpu.VMEM((half, width), F32)],
        flops=2 * flops,
        limit=24,
    )

    def update_two(own_ref, new_ref, *rest):
        parts, (change_ref, change_bf_ref) = rest[:-2], rest[-2:]
        rows = own_ref[...]
        change = rescale(new_ref[...] - summed(parts), norm(rows)) - rows
        change_ref[...] = change
        change_bf_ref[...] = change.astype(BF16)

    change, change_bf = call(update_two, [piece_f32, piece_bf], (own, new, *scatter(grads)))

    def near(change_ref, *rest):
        parts, (prefix_ref, ring_ref) = rest[:3], rest[3:]
        here = lax.axis_index("block") % 4
        prefix, ring = change_ref[...], change_ref[...]
        for k, ref in zip(RING, parts):
            part = ref[...].astype(F32)
            ring = ring + part
            prefix = prefix + jnp.where(before(here, k), part, 0.0)
        prefix_ref[...] = prefix
        ring_ref[...] = ring.astype(BF16)

    prefix, ring = call(
        near, [piece_f32, piece_bf], (change, *[along_block(change_bf, k, 1) for k in RING])
    )

    def far(own_ref, prefix_ref, *rest):
        parts, applied_ref = rest[:3], rest[3]
        here = lax.axis_index("block") // 4
        prefix, rows = prefix_ref[...], own_ref[...]
        for k, ref in zip(RING, parts):
            prefix = prefix + jnp.where(before(here, k), ref[...].astype(F32), 0.0)
        applied_ref[...] = rescale(rows + prefix, norm(rows)).astype(BF16)

    (applied,) = call(far, [piece_bf], (own, prefix, *[along_block(ring, k, 4) for k in RING]))

    mine = gather(applied)
    theirs = [swap(part) for part in mine]

    def apply_to(queries, weights):
        gate, upper = nt(queries, weights[0]), nt(queries, weights[1])
        return nn((jax.nn.silu(gate) * upper).astype(BF16), weights[2])

    def joined(part_refs):
        return [jnp.concatenate([ref[i] for ref in part_refs], 0) for i in range(3)]

    def apply_mine(queries_ref, *rest):
        weights = joined(rest[:-1])
        for at in range(0, tokens, TILE):
            rest[-1][at : at + TILE] = apply_to(queries_ref[at : at + TILE], weights)

    def apply_theirs(queries_ref, partial_ref, *rest):
        part_refs, (out_hbm, out_ref, sem) = rest[:-3], rest[-3:]
        weights = joined(part_refs)
        copies = []
        for n, at in enumerate(range(0, tokens, TILE)):
            tile = slice(at, at + TILE)
            out_ref[tile] = (partial_ref[tile] + apply_to(queries_ref[tile], weights)).astype(BF16)
            copies.append(pltpu.make_async_copy(out_ref.at[tile], out_hbm.at[tile], sem.at[n]))
            copies[-1].start()
        for copy in copies:
            copy.wait()

    (partial,) = call(apply_mine, [shape((tokens, width), F32)], (queries, *mine), flops=flops // 2, limit=24)
    (outputs,) = call(
        apply_theirs,
        [shape((tokens, width), BF16)],
        (queries, partial, *theirs),
        [pltpu.VMEM((tokens, width), BF16), pltpu.SemaphoreType.DMA((tokens // TILE,))],
        flops=flops // 2,
        limit=24,
        out_specs=[HBM],
    )
    return outputs


def solution(mesh):
    return jax.shard_map(
        shards,
        mesh=mesh,
        in_specs=(
            P(("block", "tok"), None),
            P(("block", "tok"), None),
            P(("block", "tok"), None),
            P(None, ("block", "tok")),
            P(),
        ),
        out_specs=P(("block", "tok"), None),
        check_vma=False,
    )
```
